32 devices in a mesh: dp: 16 (over z, y, core), owner: 2 (over x).
Axes of the slice: x: 2, y: 2, z: 4, core: 2. Of those that a mesh axis runs over, the one named last changes fastest.
Arguments:
- inputs: bfloat16 [2048, 8192], P('dp'), may hold values from -8 to 8
- out_grads: bfloat16 [2048, 1024], P('dp', 'owner'), may hold values from -12 to 12
- weights: float32 [32, 512, 512], P(('dp', 'owner')), may hold values from -0.0625 to 0.0625
- left_stats: float32 [32, 512, 512], P(('dp', 'owner')), as said below
- right_stats: float32 [32, 512, 512], P(('dp', 'owner')), as said below
- left_roots: float32 [32, 512, 512], P(('dp', 'owner')), as said below
- right_roots: float32 [32, 512, 512], P(('dp', 'owner')), as said below
- refresh: int32 [32], P(('dp', 'owner')), may hold values from 0 to 1, as said below
Outputs:
- new_left_stats: float32 [32, 512, 512], P(('dp', 'owner'))
- new_right_stats: float32 [32, 512, 512], P(('dp', 'owner'))
- new_left_roots: float32 [32, 512, 512], P(('dp', 'owner'))
- new_right_roots: float32 [32, 512, 512], P(('dp', 'owner'))
- update: float32 [32, 512, 512], P(('dp', 'owner'))
- queries: bfloat16 [2048, 1024], P('dp', 'owner')
The draws below stay inside these ranges and needn't reach their ends.
Inputs may be any that keep to these rules, and one draw needn't show every extreme that they name: For every k, refresh[2k] + refresh[2k + 1] is at most 1, and refresh[0] + refresh[1] is 1. `left_stats`: every block is symmetric positive definite. `right_stats`: every block is symmetric positive definite. `left_roots`: every block is symmetric positive definite. `right_roots`: every block is symmetric positive definite.
All inputs are finite; a program needn't handle non-finite values.
Results may differ from the reference program's by a relative error of at most 0.015.
Values may be sent and summed in bfloat16 or wider, within the bound.
A program may use at most 128 MiB of HBM per device.

```python
import math
import jax
import jax.numpy as jnp
from jax import lax

D = 8192
B = 512
NEWTON = 2
TOKENS = 2048
COL_DEV = 512
COLS = 1024
BLOCKS = 32
N_DP = 16
N_OWNER = 2


def definite(key, count, order):
    keys = jax.random.split(key, 2)
    noise = jax.random.normal(keys[0], (count, order, order), jnp.float32) * (0.4 / order ** 0.5)
    noise = (noise + jnp.swapaxes(noise, 1, 2)) * 0.5 ** 0.5
    diagonal = jnp.exp(jax.random.uniform(keys[1], (count, order), jnp.float32, 0.0, 1.0986))
    identity = jnp.eye(order, dtype=jnp.float32)
    matrix = noise + diagonal[:, :, None] * identity[None, :, :]
    return matrix


def draw_left_stats(key, part):
    return definite(jax.random.fold_in(key, 11), BLOCKS, B)


def draw_right_stats(key, part):
    return definite(jax.random.fold_in(key, 12), BLOCKS, B)


def draw_left_roots(key, part):
    return definite(jax.random.fold_in(key, 13), BLOCKS, B)


def draw_right_roots(key, part):
    return definite(jax.random.fold_in(key, 14), BLOCKS, B)


def draw_refresh(key, part):
    pair_count = BLOCKS // 2
    keys = jax.random.split(jax.random.fold_in(key, 21), 2)
    active = (jax.random.randint(keys[0], (pair_count,), 0, 3) > 0).astype(jnp.int32)
    active = active.at[0].set(1)
    which_one = jax.random.randint(keys[1], (pair_count,), 0, 2)
    first_flag = active * (which_one == 0).astype(jnp.int32)
    second_flag = active - first_flag
    return jnp.stack([first_flag, second_flag], 1).reshape(BLOCKS)


def raised(entries, key, source, target, shards_of, factor):
    owner, partner = [(jnp.arange(entries.shape[position]) // (entries.shape[position] // shards_of)).reshape([-1 if axis == position else 1 for axis in range(entries.ndim)]) for position in (source, target)]
    chosen = jax.random.permutation(key, shards_of)[partner]
    strong = (owner == chosen) | (owner == (partner + shards_of // 2) % shards_of)
    return jnp.where(strong, factor * entries, entries)


def levels(own_key, shape, cuts, least, top_value):
    gain, own = 1.0, jax.random.fold_in(own_key, 6)
    for axis_at, shards_of in cuts:
        heights = jnp.exp(jax.random.uniform(jax.random.fold_in(own, axis_at), (shards_of,), jnp.float32, least / len(cuts), top_value / len(cuts)))
        gain = gain * jnp.repeat(heights, shape[axis_at] // shards_of).reshape([-1 if axis == axis_at else 1 for axis in range(len(shape))])
    return gain


def bell_draw(rng, extent, scale, bound, cuts=(), held_as=jnp.bfloat16):
    values = scale * jax.random.normal(rng, extent, jnp.float32)
    if cuts:
        values = values * levels(rng, extent, cuts, -0.22, 0.18)
    return jnp.clip(values, -bound, bound).astype(held_as)


def heavy_noise(rng, dims, scale, bound, shards, heavy, kind=jnp.bfloat16):
    drawn = scale * jax.random.normal(rng, dims, jnp.float32)
    if shards:
        drawn = drawn * levels(rng, dims, shards, -0.22, 0.18)
    return jnp.clip(raised(drawn, jax.random.fold_in(rng, 3), *heavy), -bound, bound).astype(kind)


def setup_inputs(seed: int = 0) -> dict:
    seeds = jax.random.split(jax.random.key(seed), 9)
    inputs = heavy_noise(seeds[0], (TOKENS, D), 1.0, 8.0, ((0, 16),), (0, 1, 16, 2.0))
    out_grads = bell_draw(seeds[1], (TOKENS, COLS), ((TOKENS / B) ** 0.5), 12.0, ((0, 16), (1, 2)))
    weights = bell_draw(seeds[2], (BLOCKS, B, B), D ** -0.5, 0.0625, ((0, 32),), jnp.float32)
    left_stats = draw_left_stats(jax.random.fold_in(seeds[8], 71), 0)
    right_stats = draw_right_stats(jax.random.fold_in(seeds[8], 71), 0)
    left_roots = draw_left_roots(jax.random.fold_in(seeds[8], 71), 0)
    right_roots = draw_right_roots(jax.random.fold_in(seeds[8], 71), 0)
    refresh = draw_refresh(jax.random.fold_in(seeds[8], 71), 0)
    return {"inputs": inputs, "out_grads": out_grads, "weights": weights, "left_stats": left_stats, "right_stats": right_stats, "left_roots": left_roots, "right_roots": right_roots, "refresh": refresh}


BETA = 0.95
DAMPING = 0.0001
HIGHEST = lax.Precision.HIGHEST

def matmul(left_mat, right_mat):
    return jnp.dot(left_mat, right_mat, precision=HIGHEST, preferred_element_type=jnp.float32)

def inverse_root(statistic):
    identity = jnp.eye(statistic.shape[0], dtype=jnp.float32)
    damped = statistic + DAMPING * identity
    factor_z = 2.5 / jnp.sqrt(jnp.sum(damped * damped))
    current = factor_z * damped
    result = jnp.sqrt(jnp.sqrt(factor_z)) * identity
    for turn in range(NEWTON):
        factor = 1.25 * identity - 0.25 * current
        result = matmul(result, factor)
        square = matmul(factor, factor)
        current = matmul(matmul(square, square), current)
    return result

def both_roots(left_stat, right_stat, left_old, right_old):
    return (inverse_root(left_stat), inverse_root(right_stat))

def stale_roots(left_stat, right_stat, left_old, right_old):
    return (left_old, right_old)

def reference(inputs, out_grads, weights, left_stats, right_stats, left_roots, right_roots, refresh):
    tok_total = inputs.shape[0]
    tok_local = tok_total // N_DP
    row_blocks = D // B
    col_blocks = COL_DEV // B
    x_parts = inputs.reshape(N_DP, tok_local, D)
    g_parts = out_grads.reshape(N_DP, tok_local, COLS)

    def add_part(running, pieces):
        x_piece, g_piece = pieces
        product = lax.dot_general(x_piece, g_piece, (((0,), (0,)), ((), ())), preferred_element_type=jnp.float32) / tok_total
        product = lax.optimization_barrier(product.astype(jnp.bfloat16))
        return (running + product.astype(jnp.float32), None)
    grad, unused = lax.scan(add_part, jnp.zeros((D, COLS), jnp.float32), (x_parts, g_parts))
    grad_blocks = grad.reshape(row_blocks, B, N_OWNER, col_blocks, B).transpose(0, 3, 2, 1, 4).reshape(BLOCKS, B, B)
    rate = 0.25 / math.sqrt(D)

    def per_block(items):
        grad_block, weight_block, left_stat, right_stat, left_old, right_old, flag_value = items
        left_new = BETA * left_stat + (1.0 - BETA) * matmul(grad_block, grad_block.T)
        right_new = BETA * right_stat + (1.0 - BETA) * matmul(grad_block.T, grad_block)
        left_root, right_root = lax.cond(flag_value > 0, both_roots, stale_roots, left_new, right_new, left_old, right_old)
        direction = matmul(matmul(left_root, grad_block), right_root)
        direction = direction * (B / jnp.sqrt(jnp.sum(direction * direction) + 1e-12))
        updated = (weight_block - rate * direction).astype(jnp.bfloat16)
        return (left_new, right_new, left_root, right_root, direction, updated)
    outputs = lax.map(per_block, (grad_blocks, weights, left_stats, right_stats, left_roots, right_roots, refresh))
    left_new, right_new, left_root, right_root, direction, updated = outputs
    full_weight = updated.reshape(row_blocks, col_blocks, N_OWNER, B, B).transpose(0, 3, 2, 1, 4).reshape(D, COLS)
    queries = jnp.dot(inputs, full_weight, preferred_element_type=jnp.float32).astype(jnp.bfloat16)
    return (left_new, right_new, left_root, right_root, direction, queries)
```

```python
import math

import jax
import jax.numpy as jnp
from jax import lax
from jax.sharding import PartitionSpec as P

BETA = 0.95
DAMPING = 0.0001
BF16 = jnp.bfloat16
F32 = jnp.float32


def dot(a, b, dims=((1,), (0,))):
    return lax.dot_general(a.astype(BF16), b.astype(BF16), (dims, ((), ())), preferred_element_type=F32)


def split(a):
    high = a.astype(BF16)
    return high, (a - high.astype(F32)).astype(BF16)


def dot3(a, b):
    a_high, a_low = split(a)
    b_high, b_low = split(b)
    return dot(a_high, b_high) + (dot(a_high, b_low) + dot(a_low, b_high))


def inverse_root(statistic):
    eye = jnp.eye(statistic.shape[0], dtype=F32)
    damped = statistic + DAMPING * eye
    z = 2.5 / jnp.sqrt(jnp.sum(damped * damped))
    m = z * damped
    p = dot(m, m)
    r = 1.5625 * m - 0.625 * p + 0.0625 * dot(p, m)
    w = 0.0625 * r + 0.1953125 * m - 0.01953125 * p
    return jnp.sqrt(jnp.sqrt(z)) * (1.5625 * eye - 0.3125 * m - 0.48828125 * r + dot(w, r))


def roots(left_stat, right_stat, left_old, right_old):
    return (inverse_root(left_stat), inverse_root(right_stat))


def stale(left_stat, right_stat, left_old, right_old):
    return (left_old, right_old)


def body(inputs, out_grads, weights, left_stats, right_stats, left_roots, right_roots, refresh):
    tok_local, model_width = inputs.shape
    block = weights.shape[1]
    col_count = out_grads.shape[1]
    row_blocks = model_width // block
    col_blocks = col_count // block
    replicas = lax.axis_size("dp")
    tok_total = tok_local * replicas
    mine = lax.axis_index("dp") % col_blocks
    grads = lax.all_gather(out_grads, "dp", axis=0, tiled=True)
    grads = lax.dynamic_slice_in_dim(grads, mine * block, block, 1)
    send = jnp.repeat(inputs.reshape(tok_local, row_blocks, block).transpose(1, 0, 2), col_blocks, axis=0)
    features = lax.all_to_all(send, "dp", split_axis=0, concat_axis=0, tiled=True)
    features = features.reshape(tok_total, block)
    gradient = dot(features, grads, ((0,), (0,))) / tok_total
    left_new = BETA * left_stats[0] + (1.0 - BETA) * dot(gradient, gradient, ((1,), (1,)))
    right_new = BETA * right_stats[0] + (1.0 - BETA) * dot(gradient, gradient, ((0,), (0,)))
    left_root, right_root = lax.cond(
        refresh[0] > 0, roots, stale, left_new, right_new, left_roots[0], right_roots[0]
    )
    direction = dot3(dot3(left_root, gradient), right_root)
    direction = direction * (block / jnp.sqrt(jnp.sum(direction * direction) + 1e-12))
    rate = 0.25 / math.sqrt(model_width)
    updated = (weights[0] - rate * direction).astype(BF16)
    partial = dot(features, updated).astype(BF16)
    if col_blocks > 1:
        partial = lax.dynamic_update_slice(jnp.zeros((tok_total, col_count), BF16), partial, (0, mine * block))
    queries = lax.psum_scatter(partial, "dp", scatter_dimension=0, tiled=True)
    return (left_new[None], right_new[None], left_root[None], right_root[None], direction[None], queries)


def solution(mesh):
    blocks = P(("dp", "owner"), None, None)
    in_specs = (P("dp", None), P("dp", "owner"), blocks, blocks, blocks, blocks, blocks, P(("dp", "owner")))
    out_specs = (blocks,) * 5 + (P("dp", "owner"),)
    return jax.shard_map(body, mesh=mesh, in_specs=in_specs, out_specs=out_specs, check_vma=False)
```

```python
import functools
import math

import jax
import jax.numpy as jnp
from jax import lax
from jax.experimental import pallas as pl
from jax.experimental.pallas import tpu as pltpu
from jax.sharding import PartitionSpec as P

BETA = 0.95
DAMPING = 0.0001
BF16 = jnp.bfloat16
F32 = jnp.float32


def dot(a, b, dims=((1,), (0,))):
    return lax.dot_general(a.astype(BF16), b.astype(BF16), (dims, ((), ())), preferred_element_type=F32)


def split(a):
    high = a.astype(BF16)
    return high, (a - high.astype(F32)).astype(BF16)


def dot3(a, b):
    a_high, a_low = split(a)
    b_high, b_low = split(b)
    return dot(a_high, b_high) + (dot(a_high, b_low) + dot(a_low, b_high))


def inverse_root(statistic):
    eye = jnp.eye(statistic.shape[0], dtype=F32)
    damped = statistic + DAMPING * eye
    z = 2.5 / jnp.sqrt(jnp.sum(damped * damped))
    m = z * damped
    p = dot(m, m)
    r = 1.5625 * m - 0.625 * p + 0.0625 * dot(p, m)
    w = 0.0625 * r + 0.1953125 * m - 0.01953125 * p
    return jnp.sqrt(jnp.sqrt(z)) * (1.5625 * eye - 0.3125 * m - 0.48828125 * r + dot(w, r))


def roots(left_stat, right_stat, left_old, right_old):
    return (inverse_root(left_stat), inverse_root(right_stat))


def stale(left_stat, right_stat, left_old, right_old):
    return (left_old, right_old)

LINE = 4


def flip(index, stride):
    return index + stride - 2 * stride * lax.rem(lax.div(index, stride), 2)


def remote(src, dst, send, recv, peer):
    return pltpu.make_async_remote_copy(
        src_ref=src, dst_ref=dst, send_sem=send, recv_sem=recv,
        device_id=peer, device_id_type=pl.DeviceIdType.MESH,
    )


def greet(peers):
    barrier = pltpu.get_barrier_semaphore()
    for peer in peers:
        pl.semaphore_signal(barrier, inc=1, device_id=peer, device_id_type=pl.DeviceIdType.MESH)
    pl.semaphore_wait(barrier, len(peers))


def by_distance(n):
    return sorted(range(1, n), key=lambda k: -min(k, n - k))


def gather_kernel(n, x_ref, g_ref, f_ref, ga_ref, x_own, g_own, own, fs, fr, xs, xr, zs, zr, ys, yr, cs, cr):
    me, mine = lax.axis_index("dp"), lax.axis_index("owner")
    nz = n // LINE
    rows, width = g_ref.shape
    half = rows // 2
    near = pl.ds(pl.multiple_of(mine * half, half), half)
    far = pl.ds(pl.multiple_of((1 - mine) * half, half), half)
    pair, row = flip(me, 1), flip(me, 2)

    def cols(block):
        return pl.ds(pl.multiple_of(block * width, width), width)

    own_in = [
        pltpu.make_async_copy(x_ref.at[:, cols(me)], x_own, own.at[0]),
        pltpu.make_async_copy(g_ref, g_own, own.at[1]),
    ]
    for copy in own_in:
        copy.start()
    greet([(lax.rem(me + k, n), mine) for k in range(1, n)] + [(me, 1 - mine)])
    sent = []

    def go(copy):
        copy.start()
        sent.append(copy)
        return copy

    z_copy = {}
    for k in by_distance(nz):
        z_copy[k] = go(remote(g_ref, ga_ref.at[me], zs.at[k], zr.at[k], (lax.rem(me + LINE * k, n), mine)))
    f_copy = {}
    order = by_distance(n)
    for k in order:
        peer = lax.rem(me + k, n)
        f_copy[k] = go(remote(x_ref.at[near, cols(peer)], f_ref.at[me, near], fs.at[k], fr.at[k], (peer, mine)))
    y_copy, c_copy = {}, {}
    for k in [0] + by_distance(nz):
        source = lax.rem(me - LINE * k + n, n)
        if k:
            z_copy[k].wait_recv()
        block = ga_ref.at[source] if k else g_ref
        y_copy[k] = go(remote(block, ga_ref.at[source], ys.at[k], yr.at[k], (row, mine)))
        c_copy[k] = go(remote(block, ga_ref.at[source], cs.at[k], cr.at[k], (pair, mine)))
    own_out = [
        pltpu.make_async_copy(x_own, f_ref.at[me], own.at[2]),
        pltpu.make_async_copy(g_own, ga_ref.at[me], own.at[3]),
    ]
    for first, second in zip(own_in, own_out):
        first.wait()
        second.start()
    x_copy = {}

    def pass_on(k):
        f_copy[k].wait_recv()
        held = f_ref.at[lax.rem(me - k + n, n), near]
        x_copy[k] = go(remote(held, held, xs.at[k], xr.at[k], (me, 1 - mine)))

    quick = order[::-1]
    for at, k in enumerate([0] + by_distance(nz)):
        y_copy[k].wait_recv()
        source = lax.rem(row - LINE * k + n, n)
        block = ga_ref.at[source]
        c_copy[nz + k] = go(remote(block, block, cs.at[nz + k], cr.at[nz + k], (pair, mine)))
    for k in quick:
        pass_on(k)
    for k in range(2 * nz):
        c_copy[k].wait_recv()
    for k in quick:
        x_copy[k].wait_recv()
    for copy in own_out:
        copy.wait()
    for copy in sent:
        copy.wait_send()


def gather(n, inputs, out_grads):
    rows, width = out_grads.shape
    nz = n // LINE
    dma = pltpu.SemaphoreType.DMA
    anywhere = pl.BlockSpec(memory_space=pl.ANY)
    return pl.pallas_call(
        functools.partial(gather_kernel, n),
        out_shape=[jax.ShapeDtypeStruct((n, rows, width), BF16)] * 2,
        in_specs=[anywhere] * 2,
        out_specs=[anywhere] * 2,
        scratch_shapes=[pltpu.VMEM((rows, width), BF16)] * 2
        + [dma((4,))] + [dma((n,))] * 4 + [dma((nz,))] * 4 + [dma((2 * nz,))] * 2,
        compiler_params=pltpu.CompilerParams(collective_id=0, has_side_effects=True),
        name="gather_blocks",
    )(inputs, out_grads)


def reduce_kernel(n, f_ref, w_ref, q_ref, a_out, a_in, b_out, b_in, c_out, c_in, total, a_s, a_r, b_s, b_r, c_s, c_r):
    me, mine = lax.axis_index("dp"), lax.axis_index("owner")
    nz = n // LINE
    pair, row = flip(me, 1), flip(me, 2)
    order = by_distance(nz) + [0]
    greet([(pair, mine), (row, mine)] + [(lax.rem(me + LINE * k, n), mine) for k in range(1, nz)])

    def part(block):
        return jnp.dot(f_ref[block], w_ref[...], preferred_element_type=F32)

    sent = []

    def go(copy):
        copy.start()
        sent.append(copy)
        return copy

    a_copy, b_copy, c_copy = {}, {}, {}
    for k in order:
        for turn, base in ((1, flip(row, 1)), (0, pair)):
            at = 2 * k + turn
            a_out[at] = part(lax.rem(base + LINE * k, n)).astype(BF16)
            a_copy[at] = go(remote(a_out.at[at], a_in.at[at], a_s.at[at], a_r.at[at], (pair, mine)))
    for k in order:
        mine_part = part(lax.rem(row + LINE * k, n))
        a_copy[2 * k + 1].wait_recv()
        b_out[k] = (mine_part + a_in[2 * k + 1].astype(F32)).astype(BF16)
        b_copy[k] = go(remote(b_out.at[k], b_in.at[k], b_s.at[k], b_r.at[k], (row, mine)))
    for k in order:
        total[k] = part(lax.rem(me + LINE * k, n))
        a_copy[2 * k].wait_recv()
        total[k] += a_in[2 * k].astype(F32)
    for k in order:
        b_copy[k].wait_recv()
        if k:
            c_out[k] = (total[k] + b_in[k].astype(F32)).astype(BF16)
            peer = lax.rem(me + LINE * k, n)
            c_copy[k] = go(remote(c_out.at[k], c_in.at[k], c_s.at[k], c_r.at[k], (peer, mine)))
    result = total[0] + b_in[0].astype(F32)
    for k in by_distance(nz)[::-1]:
        c_copy[k].wait_recv()
        result = result + c_in[k].astype(F32)
    q_ref[...] = result.astype(BF16)
    for copy in sent:
        copy.wait_send()


def reduce_queries(n, features, updated):
    rows, width = features.shape[1], updated.shape[1]
    nz = n // LINE
    dma = pltpu.SemaphoreType.DMA
    vmem = pl.BlockSpec(memory_space=pltpu.VMEM)
    return pl.pallas_call(
        functools.partial(reduce_kernel, n),
        out_shape=jax.ShapeDtypeStruct((rows, width), BF16),
        in_specs=[vmem] * 2,
        out_specs=vmem,
        scratch_shapes=[pltpu.VMEM((2 * nz, rows, width), BF16)] * 2
        + [pltpu.VMEM((nz, rows, width), BF16)] * 4
        + [pltpu.VMEM((nz, rows, width), F32)]
        + [dma((2 * nz,))] * 2 + [dma((nz,))] * 4,
        compiler_params=pltpu.CompilerParams(collective_id=1, has_side_effects=True),
        name="reduce_queries",
    )(features, updated)


def body(inputs, out_grads, weights, left_stats, right_stats, left_roots, right_roots, refresh):
    tok_local, model_width = inputs.shape
    block = weights.shape[1]
    col_count = out_grads.shape[1]
    row_blocks = model_width // block
    col_blocks = col_count // block
    replicas = lax.axis_size("dp")
    tok_total = tok_local * replicas
    kernels = col_blocks == 1 and lax.axis_size("owner") == 2 and replicas % LINE == 0
    if kernels:
        features, grads = gather(replicas, inputs, out_grads)
        features = features.reshape(tok_total, block)
        grads = grads.reshape(tok_total, block)
    else:
        mine = lax.axis_index("dp") % col_blocks
        grads = lax.all_gather(out_grads, "dp", axis=0, tiled=True)
        grads = lax.dynamic_slice_in_dim(grads, mine * block, block, 1)
        send = jnp.repeat(inputs.reshape(tok_local, row_blocks, block).transpose(1, 0, 2), col_blocks, axis=0)
        features = lax.all_to_all(send, "dp", split_axis=0, concat_axis=0, tiled=True)
        features = features.reshape(tok_total, block)
    gradient = dot(features, grads, ((0,), (0,))) / tok_total
    left_new = BETA * left_stats[0] + (1.0 - BETA) * dot(gradient, gradient, ((1,), (1,)))
    right_new = BETA * right_stats[0] + (1.0 - BETA) * dot(gradient, gradient, ((0,), (0,)))
    left_root, right_root = lax.cond(
        refresh[0] > 0, roots, stale, left_new, right_new, left_roots[0], right_roots[0]
    )
    direction = dot3(dot3(left_root, gradient), right_root)
    direction = direction * (block / jnp.sqrt(jnp.sum(direction * direction) + 1e-12))
    rate = 0.25 / math.sqrt(model_width)
    updated = (weights[0] - rate * direction).astype(BF16)
    if kernels:
        queries = reduce_queries(replicas, features.reshape(replicas, tok_local, block), updated)
    else:
        partial = dot(features, updated).astype(BF16)
        if col_blocks > 1:
            partial = lax.dynamic_update_slice(jnp.zeros((tok_total, col_count), BF16), partial, (0, mine * block))
        queries = lax.psum_scatter(partial, "dp", scatter_dimension=0, tiled=True)
    return (left_new[None], right_new[None], left_root[None], right_root[None], direction[None], queries)


def solution(mesh):
    blocks = P(("dp", "owner"), None, None)
    in_specs = (P("dp", None), P("dp", "owner"), blocks, blocks, blocks, blocks, blocks, P(("dp", "owner")))
    out_specs = (blocks,) * 5 + (P("dp", "owner"),)
    return jax.shard_map(body, mesh=mesh, in_specs=in_specs, out_specs=out_specs, check_vma=False)
```

```python
import functools
import math

import jax
import jax.numpy as jnp
from jax import lax
from jax.experimental import pallas as pl
from jax.experimental.pallas import tpu as pltpu
from jax.sharding import PartitionSpec as P

BETA = 0.95
DAMPING = 0.0001
BF16 = jnp.bfloat16
F32 = jnp.float32


def dot(a, b, dims=((1,), (0,))):
    return lax.dot_general(a.astype(BF16), b.astype(BF16), (dims, ((), ())), preferred_element_type=F32)


def split(a):
    high = a.astype(BF16)
    return high, (a - high.astype(F32)).astype(BF16)


def dot3(a, b):
    a_high, a_low = split(a)
    b_high, b_low = split(b)
    return dot(a_high, b_high) + (dot(a_high, b_low) + dot(a_low, b_high))


def inverse_root(statistic):
    shape = statistic.shape
    eye = (lax.broadcasted_iota(jnp.int32, shape, 0) == lax.broadcasted_iota(jnp.int32, shape, 1)).astype(F32)
    damped = statistic + DAMPING * eye
    z = 2.5 / jnp.sqrt(jnp.sum(damped * damped, keepdims=True))
    m = z * damped
    p = dot(m, m)
    r = 1.5625 * m - 0.625 * p + 0.0625 * dot(p, m)
    w = 0.0625 * r + 0.1953125 * m - 0.01953125 * p
    return jnp.sqrt(jnp.sqrt(z)) * (1.5625 * eye - 0.3125 * m - 0.48828125 * r + dot(w, r))


def roots(left_stat, right_stat, left_old, right_old):
    return (inverse_root(left_stat), inverse_root(right_stat))


def stale(left_stat, right_stat, left_old, right_old):
    return (left_old, right_old)

LINE = 4


def flip(index, stride):
    return index + stride - 2 * stride * lax.rem(lax.div(index, stride), 2)


def remote(src, dst, send, recv, peer):
    return pltpu.make_async_remote_copy(
        src_ref=src, dst_ref=dst, send_sem=send, recv_sem=recv,
        device_id=peer, device_id_type=pl.DeviceIdType.MESH,
    )


def greet(peers):
    barrier = pltpu.get_barrier_semaphore()
    for peer in peers:
        pl.semaphore_signal(barrier, inc=1, device_id=peer, device_id_type=pl.DeviceIdType.MESH)
    pl.semaphore_wait(barrier, len(peers))


def by_distance(n):
    return sorted(range(1, n), key=lambda k: -min(k, n - k))


def gather_kernel(n, x_ref, g_ref, f_ref, ga_ref, x_own, g_own, own, fs, fr, xs, xr, zs, zr, ys, yr, cs, cr):
    me, mine = lax.axis_index("dp"), lax.axis_index("owner")
    nz = n // LINE
    rows, width = g_ref.shape
    half = rows // 2
    near = pl.ds(pl.multiple_of(mine * half, half), half)
    far = pl.ds(pl.multiple_of((1 - mine) * half, half), half)
    pair, row = flip(me, 1), flip(me, 2)

    def cols(block):
        return pl.ds(pl.multiple_of(block * width, width), width)

    own_in = [
        pltpu.make_async_copy(x_ref.at[:, cols(me)], x_own, own.at[0]),
        pltpu.make_async_copy(g_ref, g_own, own.at[1]),
    ]
    for copy in own_in:
        copy.start()
    greet([(lax.rem(me + k, n), mine) for k in range(1, n)] + [(me, 1 - mine)])
    sent = []

    def go(copy):
        copy.start()
        sent.append(copy)
        return copy

    z_copy = {}
    for k in by_distance(nz):
        z_copy[k] = go(remote(g_ref, ga_ref.at[me], zs.at[k], zr.at[k], (lax.rem(me + LINE * k, n), mine)))
    f_copy = {}
    order = by_distance(n)
    for k in order:
        peer = lax.rem(me + k, n)
        f_copy[k] = go(remote(x_ref.at[near, cols(peer)], f_ref.at[me, near], fs.at[k], fr.at[k], (peer, mine)))
    y_copy, c_copy = {}, {}
    for k in [0] + by_distance(nz):
        source = lax.rem(me - LINE * k + n, n)
        if k:
            z_copy[k].wait_recv()
        block = ga_ref.at[source] if k else g_ref
        y_copy[k] = go(remote(block, ga_ref.at[source], ys.at[k], yr.at[k], (row, mine)))
        c_copy[k] = go(remote(block, ga_ref.at[source], cs.at[k], cr.at[k], (pair, mine)))
    own_out = [
        pltpu.make_async_copy(x_own, f_ref.at[me], own.at[2]),
        pltpu.make_async_copy(g_own, ga_ref.at[me], own.at[3]),
    ]
    for first, second in zip(own_in, own_out):
        first.wait()
        second.start()
    x_copy = {}

    def pass_on(k):
        f_copy[k].wait_recv()
        held = f_ref.at[lax.rem(me - k + n, n), near]
        x_copy[k] = go(remote(held, held, xs.at[k], xr.at[k], (me, 1 - mine)))

    quick = order[::-1]
    for at, k in enumerate([0] + by_distance(nz)):
        y_copy[k].wait_recv()
        source = lax.rem(row - LINE * k + n, n)
        block = ga_ref.at[source]
        c_copy[nz + k] = go(remote(block, block, cs.at[nz + k], cr.at[nz + k], (pair, mine)))
    for k in quick:
        pass_on(k)
    for k in range(2 * nz):
        c_copy[k].wait_recv()
    for k in quick:
        x_copy[k].wait_recv()
    for copy in own_out:
        copy.wait()
    for copy in sent:
        copy.wait_send()


def gather(n, inputs, out_grads):
    rows, width = out_grads.shape
    nz = n // LINE
    dma = pltpu.SemaphoreType.DMA
    anywhere = pl.BlockSpec(memory_space=pl.ANY)
    return pl.pallas_call(
        functools.partial(gather_kernel, n),
        out_shape=[jax.ShapeDtypeStruct((n, rows, width), BF16)] * 2,
        in_specs=[anywhere] * 2,
        out_specs=[anywhere] * 2,
        scratch_shapes=[pltpu.VMEM((rows, width), BF16)] * 2
        + [dma((4,))] + [dma((n,))] * 4 + [dma((nz,))] * 4 + [dma((2 * nz,))] * 2,
        compiler_params=pltpu.CompilerParams(collective_id=0, has_side_effects=True),
        name="gather_blocks",
    )(inputs, out_grads)


def reduce_kernel(n, f_ref, w_ref, q_ref, a_out, a_in, b_out, b_in, c_out, c_in, total, a_s, a_r, b_s, b_r, c_s, c_r):
    me, mine = lax.axis_index("dp"), lax.axis_index("owner")
    nz = n // LINE
    pair, row = flip(me, 1), flip(me, 2)
    order = by_distance(nz) + [0]
    greet([(pair, mine), (row, mine)] + [(lax.rem(me + LINE * k, n), mine) for k in range(1, nz)])

    def part(block):
        return jnp.dot(f_ref[block], w_ref[...], preferred_element_type=F32)

    sent = []

    def go(copy):
        copy.start()
        sent.append(copy)
        return copy

    a_copy, b_copy, c_copy = {}, {}, {}
    for k in order:
        for turn, base in ((1, flip(row, 1)), (0, pair)):
            at = 2 * k + turn
            a_out[at] = part(lax.rem(base + LINE * k, n)).astype(BF16)
            a_copy[at] = go(remote(a_out.at[at], a_in.at[at], a_s.at[at], a_r.at[at], (pair, mine)))
    for k in order:
        mine_part = part(lax.rem(row + LINE * k, n))
        a_copy[2 * k + 1].wait_recv()
        b_out[k] = (mine_part + a_in[2 * k + 1].astype(F32)).astype(BF16)
        b_copy[k] = go(remote(b_out.at[k], b_in.at[k], b_s.at[k], b_r.at[k], (row, mine)))
    for k in order:
        total[k] = part(lax.rem(me + LINE * k, n))
        a_copy[2 * k].wait_recv()
        total[k] += a_in[2 * k].astype(F32)
    for k in order:
        b_copy[k].wait_recv()
        if k:
            c_out[k] = (total[k] + b_in[k].astype(F32)).astype(BF16)
            peer = lax.rem(me + LINE * k, n)
            c_copy[k] = go(remote(c_out.at[k], c_in.at[k], c_s.at[k], c_r.at[k], (peer, mine)))
    result = total[0] + b_in[0].astype(F32)
    for k in by_distance(nz)[::-1]:
        c_copy[k].wait_recv()
        result = result + c_in[k].astype(F32)
    q_ref[...] = result.astype(BF16)
    for copy in sent:
        copy.wait_send()


def reduce_queries(n, features, updated):
    rows, width = features.shape[1], updated.shape[1]
    nz = n // LINE
    dma = pltpu.SemaphoreType.DMA
    vmem = pl.BlockSpec(memory_space=pltpu.VMEM)
    return pl.pallas_call(
        functools.partial(reduce_kernel, n),
        out_shape=jax.ShapeDtypeStruct((rows, width), BF16),
        in_specs=[vmem] * 2,
        out_specs=vmem,
        scratch_shapes=[pltpu.VMEM((2 * nz, rows, width), BF16)] * 2
        + [pltpu.VMEM((nz, rows, width), BF16)] * 4
        + [pltpu.VMEM((nz, rows, width), F32)]
        + [dma((2 * nz,))] * 2 + [dma((nz,))] * 4,
        compiler_params=pltpu.CompilerParams(collective_id=1, has_side_effects=True),
        name="reduce_queries",
    )(features, updated)


def step_kernel(chunks, tok_total, rate, flag, f_hbm, g_hbm, w_hbm, ls_hbm, rs_hbm, lr_hbm, rr_hbm,
                ls_out, rs_out, lr_out, rr_out, d_out, u_ref,
                f, g, w, ls, rs, lr, rr, d, grad, f_sem, g_sem, in_sem, out_sem):
    span = f.shape[0] // chunks
    pieces = []
    for k in range(chunks):
        part = pl.ds(k * span, span)
        pieces.append((
            pltpu.make_async_copy(f_hbm.at[part], f.at[part], f_sem.at[k]),
            pltpu.make_async_copy(g_hbm.at[part], g.at[part], g_sem.at[k]),
        ))
        for copy in pieces[-1]:
            copy.start()
    ins = [
        pltpu.make_async_copy(src.at[0], dst, in_sem.at[k])
        for k, (src, dst) in enumerate(((ls_hbm, ls), (rs_hbm, rs), (lr_hbm, lr), (rr_hbm, rr), (w_hbm, w)))
    ]
    for copy in ins:
        copy.start()
    outs = [
        pltpu.make_async_copy(src, dst.at[0], out_sem.at[k])
        for k, (src, dst) in enumerate(((ls, ls_out), (rs, rs_out), (lr, lr_out), (rr, rr_out), (d, d_out)))
    ]
    for k, pair in enumerate(pieces):
        for copy in pair:
            copy.wait()
        part = pl.ds(k * span, span)
        term = dot(f[part], g[part], ((0,), (0,))) * (1.0 / tok_total)
        grad[...] = term if k == 0 else grad[...] + term
    high = grad[...].astype(BF16)
    ins[0].wait()
    ls[...] = BETA * ls[...] + (1.0 - BETA) * dot(high, high, ((1,), (1,)))
    outs[0].start()
    ins[1].wait()
    rs[...] = BETA * rs[...] + (1.0 - BETA) * dot(high, high, ((0,), (0,)))
    outs[1].start()
    ins[2].wait()
    ins[3].wait()

    @pl.when(flag[0] > 0)
    def _():
        lr[...] = inverse_root(ls[...])
        rr[...] = inverse_root(rs[...])

    outs[2].start()
    outs[3].start()
    direction = dot3(dot3(lr[...], grad[...]), rr[...])
    norm = jnp.sqrt(jnp.sum(direction * direction, keepdims=True) + 1e-12)
    direction = direction * (direction.shape[0] / norm)
    d[...] = direction
    outs[4].start()
    ins[4].wait()
    u_ref[...] = (w[...] - rate * direction).astype(BF16)
    for copy in outs:
        copy.wait()


def owner_step(tok_total, rate, features, grads, weights, left_stats, right_stats, left_roots, right_roots, refresh):
    block = weights.shape[1]
    chunks = 4
    dma = pltpu.SemaphoreType.DMA
    anywhere = pl.BlockSpec(memory_space=pl.ANY)
    square = pltpu.VMEM((block, block), F32)
    return pl.pallas_call(
        functools.partial(step_kernel, chunks, tok_total, rate),
        out_shape=[jax.ShapeDtypeStruct((1, block, block), F32)] * 5 + [jax.ShapeDtypeStruct((block, block), BF16)],
        in_specs=[pl.BlockSpec(memory_space=pltpu.SMEM)] + [anywhere] * 7,
        out_specs=[anywhere] * 5 + [pl.BlockSpec(memory_space=pltpu.VMEM)],
        scratch_shapes=[pltpu.VMEM(features.shape, BF16)] * 2 + [square] * 7
        + [dma((chunks,))] * 2 + [dma((5,))] * 2,
        compiler_params=pltpu.CompilerParams(vmem_limit_bytes=56 << 20),
        name="owner_step",
    )(refresh, features, grads, weights, left_stats, right_stats, left_roots, right_roots)


def body(inputs, out_grads, weights, left_stats, right_stats, left_roots, right_roots, refresh):
    tok_local, model_width = inputs.shape
    block = weights.shape[1]
    col_count = out_grads.shape[1]
    row_blocks = model_width // block
    col_blocks = col_count // block
    replicas = lax.axis_size("dp")
    tok_total = tok_local * replicas
    kernels = col_blocks == 1 and lax.axis_size("owner") == 2 and replicas % LINE == 0
    rate = 0.25 / math.sqrt(model_width)
    if kernels:
        features, grads = gather(replicas, inputs, out_grads)
        outs = owner_step(
            tok_total, rate, features.reshape(tok_total, block), grads.reshape(tok_total, block),
            weights, left_stats, right_stats, left_roots, right_roots, refresh,
        )
        return (*outs[:5], reduce_queries(replicas, features, outs[5]))
    mine = lax.axis_index("dp") % col_blocks
    grads = lax.all_gather(out_grads, "dp", axis=0, tiled=True)
    grads = lax.dynamic_slice_in_dim(grads, mine * block, block, 1)
    send = jnp.repeat(inputs.reshape(tok_local, row_blocks, block).transpose(1, 0, 2), col_blocks, axis=0)
    features = lax.all_to_all(send, "dp", split_axis=0, concat_axis=0, tiled=True)
    features = features.reshape(tok_total, block)
    gradient = dot(features, grads, ((0,), (0,))) / tok_total
    left_new = BETA * left_stats[0] + (1.0 - BETA) * dot(gradient, gradient, ((1,), (1,)))
    right_new = BETA * right_stats[0] + (1.0 - BETA) * dot(gradient, gradient, ((0,), (0,)))
    left_root, right_root = lax.cond(
        refresh[0] > 0, roots, stale, left_new, right_new, left_roots[0], right_roots[0]
    )
    direction = dot3(dot3(left_root, gradient), right_root)
    direction = direction * (block / jnp.sqrt(jnp.sum(direction * direction) + 1e-12))
    updated = (weights[0] - rate * direction).astype(BF16)
    partial = dot(features, updated).astype(BF16)
    if col_blocks > 1:
        partial = lax.dynamic_update_slice(jnp.zeros((tok_total, col_count), BF16), partial, (0, mine * block))
    queries = lax.psum_scatter(partial, "dp", scatter_dimension=0, tiled=True)
    return (left_new[None], right_new[None], left_root[None], right_root[None], direction[None], queries)


def solution(mesh):
    blocks = P(("dp", "owner"), None, None)
    in_specs = (P("dp", None), P("dp", "owner"), blocks, blocks, blocks, blocks, blocks, P(("dp", "owner")))
    out_specs = (blocks,) * 5 + (P("dp", "owner"),)
    return jax.shard_map(body, mesh=mesh, in_specs=in_specs, out_specs=out_specs, check_vma=False)
```
